256 devices in a mesh: group: 8 (over y, core), dom: 32 (over z, x).
Axes of the slice: x: 4, y: 4, z: 8, core: 2. Of those that a mesh axis runs over, the one named last changes fastest.
Arguments:
- node_feats: bfloat16 [524288, 512], P(('group', 'dom')), may hold values from -36 to 36
- send_rows: int32 [256, 32, 32], P(('group', 'dom')), may hold values from 0 to 2047
- hub_rows: int32 [256, 8], P(('group', 'dom')), may hold values from 0 to 2047
- neighbours: int32 [524288, 16], P(('group', 'dom')), may hold values from 0 to 5119, as said below
- w_self: bfloat16 [512, 512], replicated, may hold values from -0.25 to 0.25
- w_neigh: bfloat16 [512, 512], replicated, may hold values from -0.25 to 0.25
- w_head: bfloat16 [512, 128], replicated, may hold values from -1.5 to 1.5
- s_first: bfloat16 [512, 512], replicated, may hold values from -0.25 to 0.25
- s_second: bfloat16 [512, 128], replicated, may hold values from -1.5 to 1.5
Outputs:
- teacher_hidden: bfloat16 [524288, 512], P(('group', 'dom'))
- grad_first: float32 [512, 512], replicated
- grad_second: float32 [512, 128], replicated
The draws below stay inside these ranges and needn't reach their ends.
Inputs may be any that keep to these rules, and one draw needn't show every extreme that they name: `neighbours`: entries below 2048 are local rows; entries from 2048 to 3071 name halo rows, and from a given peer only its first rows, up to 32; the rest name hubs.
All inputs are finite; a program needn't handle non-finite values.
Results may differ from the reference program's by a relative error of at most 0.0025.
Values may be sent and summed in bfloat16 or wider, within the bound.
No kernel may reach another device: no remote copies, remote signals or barrier semaphores. Data moves between devices by JAX's collectives and lax.ppermute only.
A program may use at most 128 MiB of HBM per device.

```python
import jax
import jax.numpy as jnp
from jax import lax

D = 512
HID = 512
CLASSES = 128
DEG = 16
NODE_DEV = 2048
CAP = 32
HUB_DEV = 8
SHARDS = 256
NODES = 524288
HUBS = 2048
N_GROUP = 8
N_DOM = 32


def draw_neighbours(key, part):
    shards = NODES // NODE_DEV
    keys = jax.random.split(key, 6)
    counts = jax.random.randint(keys[0], (shards, N_DOM), 1, CAP + 1)
    own_slot = jnp.arange(shards) % N_DOM
    forced = jnp.arange(N_DOM)[None, :] == ((own_slot + 1) % N_DOM)[:, None]
    counts = jnp.where(forced, CAP, counts)
    device = jnp.arange(NODES) // NODE_DEV
    group_id = device // N_DOM
    slot = device % N_DOM
    kind = jax.random.randint(keys[1], (NODES, DEG), 0, 4)
    local = jax.random.randint(keys[2], (NODES, DEG), 0, NODE_DEV)
    source = jax.random.randint(keys[3], (NODES, DEG), 0, N_DOM)
    source_dev = group_id[:, None] * N_DOM + source
    limit = counts[source_dev, jnp.broadcast_to(slot[:, None], (NODES, DEG))]
    offset = jax.random.randint(keys[4], (NODES, DEG), 0, 1048576) % limit
    halo = NODE_DEV + source * CAP + offset
    hub = NODE_DEV + N_DOM * CAP + jax.random.randint(keys[5], (NODES, DEG), 0, HUBS)
    picked = jnp.where(kind < 2, local, jnp.where(kind == 2, halo, hub))
    return picked.astype(jnp.int32)


def draw_node_feats(key, part):
    keys = jax.random.split(key, 1)
    base = jnp.clip(jax.random.normal(keys[0], (NODES, D), jnp.float32), -6.0, 6.0)
    return base.astype(jnp.bfloat16)


def classifier_draw(key, rows, cols):
    keys = jax.random.split(key, 1)
    base = jnp.clip(0.15 * jax.random.normal(keys[0], (rows, cols), jnp.float32), -0.9, 0.9)
    return base.astype(jnp.bfloat16)


def draw_w_head(key, part):
    return classifier_draw(jax.random.fold_in(key, 11), D, CLASSES)


def draw_s_second(key, part):
    return classifier_draw(jax.random.fold_in(key, 23), HID, CLASSES)


def plant(values, rng, low, largest):
    longest = values.shape.index(max(values.shape))
    spots = []
    for shift in (0, 1):
        where = [jax.random.randint(jax.random.fold_in(rng, axis), (), 0, length) for axis, length in enumerate(values.shape)]
        where[longest] = (where[longest] + shift) % values.shape[longest]
        spots.append(tuple(where))
    return values.at[spots[0]].set(low).at[spots[1]].set(largest)


def bell_draw(key, extent, spread, bound, held_as=jnp.bfloat16):
    array = spread * jax.random.normal(key, extent, jnp.float32)
    return jnp.clip(array, min=-bound, max=bound).astype(held_as)


def setup_inputs(seed: int = 0) -> dict:
    key_of = jax.random.split(jax.random.key(seed), 10)
    return {
        "node_feats": draw_node_feats(jax.random.fold_in(key_of[9], 71), 0),
        "send_rows": plant(jax.random.randint(key_of[1], (SHARDS, N_DOM, CAP), 0, NODE_DEV), jax.random.fold_in(key_of[1], 1), 0, NODE_DEV - 1).astype(jnp.int32),
        "hub_rows": plant(jax.random.randint(key_of[2], (SHARDS, HUB_DEV), 0, NODE_DEV), jax.random.fold_in(key_of[2], 1), 0, NODE_DEV - 1).astype(jnp.int32),
        "neighbours": draw_neighbours(jax.random.fold_in(key_of[9], 71), 0),
        "w_self": bell_draw(key_of[4], (D, D), D ** -0.5, 0.25),
        "w_neigh": bell_draw(key_of[5], (D, D), D ** -0.5, 0.25),
        "w_head": draw_w_head(jax.random.fold_in(key_of[9], 71), 0),
        "s_first": bell_draw(key_of[7], (D, HID), D ** -0.5, 0.25),
        "s_second": draw_s_second(jax.random.fold_in(key_of[9], 71), 0),
    }


TEMPER = 2.0

def local_layer(feats, table, nbr, w_self, w_neigh, w_head, s_first, s_second, scale):
    rows = feats.shape[0]
    block = min(512, rows)

    def agg_block(index):
        picked = table[index].astype(jnp.float32)
        return (lax.optimization_barrier(jnp.sum(picked, axis=1)) / DEG).astype(jnp.bfloat16)
    agg = lax.map(agg_block, nbr.reshape(rows // block, block, DEG)).reshape(rows, feats.shape[1])
    pre = jnp.dot(feats, w_self, preferred_element_type=jnp.float32) + jnp.dot(agg, w_neigh, preferred_element_type=jnp.float32)
    hidden = jax.nn.relu(pre).astype(jnp.bfloat16)
    t_logits = jnp.dot(hidden, w_head, preferred_element_type=jnp.float32)
    s_pre = jnp.dot(feats, s_first, preferred_element_type=jnp.float32)
    s_hidden = jax.nn.relu(s_pre).astype(jnp.bfloat16)
    s_logits = jnp.dot(s_hidden, s_second, preferred_element_type=jnp.float32)
    p_teach = jax.nn.softmax(t_logits / TEMPER, axis=-1)
    p_stud = jax.nn.softmax(s_logits / TEMPER, axis=-1)
    delta = (TEMPER * (p_stud - p_teach) * scale).astype(jnp.bfloat16)
    g_second = jnp.dot(s_hidden.T, delta, preferred_element_type=jnp.float32)
    back = jnp.dot(delta, s_second.T, preferred_element_type=jnp.float32)
    back = jnp.where(s_pre > 0, back, 0.0).astype(jnp.bfloat16)
    g_first = jnp.dot(feats.T, back, preferred_element_type=jnp.float32)
    return (hidden, g_first, g_second)

def reference(node_feats, send_rows, hub_rows, neighbours, w_self, w_neigh, w_head, s_first, s_second):
    shards = N_GROUP * N_DOM
    feats = node_feats.reshape(shards, NODE_DEV, D)
    hubs = jax.vmap(lambda f, r: f[r])(feats, hub_rows).reshape(HUBS, D)
    scale = 1.0 / jnp.sqrt(jnp.float32(NODES))

    def per_part(carry, dev):
        group_id = dev // N_DOM
        slot = dev % N_DOM
        sources = group_id * N_DOM + jnp.arange(N_DOM, dtype=jnp.int32)
        halo = jax.vmap(lambda s: feats[s][send_rows[s, slot]])(sources).reshape(N_DOM * CAP, D)
        table = jnp.concatenate([feats[dev], halo, hubs], axis=0)
        nbr = lax.dynamic_slice_in_dim(neighbours, (dev * NODE_DEV).astype(jnp.int32), NODE_DEV, 0)
        hidden, g_first, g_second = local_layer(feats[dev], table, nbr, w_self, w_neigh, w_head, s_first, s_second, scale)
        return ((carry[0] + g_first, carry[1] + g_second), hidden)
    init = (jnp.zeros((D, HID), jnp.float32), jnp.zeros((HID, CLASSES), jnp.float32))
    (grad_first, grad_second), hidden = lax.scan(per_part, init, jnp.arange(shards, dtype=jnp.int32))
    return (hidden.reshape(NODES, D), grad_first, grad_second)
```

```python
import functools

import jax
import jax.numpy as jnp
from jax import lax
from jax.experimental import pallas as pl
from jax.experimental.pallas import tpu as pltpu
from jax.sharding import Mesh
from jax.sharding import PartitionSpec as P

DEG = 16
TEMPER = 2.0
NY, NC, NZ, NX = 4, 2, 8, 4
ALL = ("y", "core", "z", "x")
DOM = ("z", "x")
YCX = ("y", "core", "x")
BF = jnp.bfloat16
F32 = jnp.float32
NT = (((1,), (1,)), ((), ()))
TN = (((0,), (0,)), ((), ()))

ROWS = 2048
WIDTH = 512
PEERS = 32
CAP = 32
HUBD = 8
SLOT = CAP + HUBD
LO = 256
LOCAL_HI = ROWS // LO
REM_HI = 12
GROUP = 16
TILE = 512


def onehot(cond):
    return jnp.where(cond, 1.0, 0.0).astype(BF)


def send_kernel(rows_ref, hub_ref, x_ref, out_ref):
    x = x_ref[...]
    rows_t = rows_ref[...].T
    lane = lax.broadcasted_iota(jnp.int32, (CAP, ROWS), 1)
    per = 8
    for block in range(PEERS // per):
        picks = jnp.concatenate(
            [onehot(rows_t[:, s : s + 1] == lane) for s in range(block * per, (block + 1) * per)], axis=0
        )
        got = jnp.dot(picks, x, preferred_element_type=F32).astype(BF)
        for n in range(per):
            out_ref[block * per + n, 0:CAP, :] = got[n * CAP : (n + 1) * CAP, :]
    hub_t = hub_ref[...].T
    hub_lane = lax.broadcasted_iota(jnp.int32, (HUBD, ROWS), 1)
    hubs = jnp.dot(onehot(hub_t[:, 0:1] == hub_lane), x, preferred_element_type=F32).astype(BF)
    for s in range(PEERS):
        out_ref[s, CAP:SLOT, :] = hubs


def send_rows_of(feats, send_rows, hub_rows):
    return pl.pallas_call(
        send_kernel,
        out_shape=jax.ShapeDtypeStruct((PEERS, SLOT, WIDTH), BF),
        compiler_params=pltpu.CompilerParams(vmem_limit_bytes=40 << 20),
        name="send_rows",
    )(send_rows, hub_rows, feats)


def local_kernel(
    idx_ref, x_ref, xall_ref, wself_ref, sfirst_ref, ssecond_ref,
    agg_ref, rem_ref, base_ref, sh_ref, ps_ref, loc_ref,
):
    high = (LOCAL_HI + REM_HI) * GROUP
    left_row = lax.broadcasted_iota(jnp.int32, (high, LO), 0)
    low_row = lax.broadcasted_iota(jnp.int32, (LO, LO), 0)
    node = lax.broadcasted_iota(jnp.int32, (1, LO), 1) // DEG

    def build(g, carry):
        idx = idx_ref[pl.ds(g, 1), :]
        where_hi = (idx // LO) * GROUP + node
        where_lo = idx % LO
        left = onehot(jnp.broadcast_to(where_hi, (high, LO)) == left_row)
        low = onehot(jnp.broadcast_to(where_lo, (LO, LO)) == low_row)
        counts = lax.dot_general(left, low, NT, preferred_element_type=F32).astype(BF)
        at = pl.ds(pl.multiple_of(g * GROUP, GROUP), GROUP)
        for h in range(LOCAL_HI):
            loc_ref[at, h * LO : (h + 1) * LO] = counts[h * GROUP : (h + 1) * GROUP, :]
        for h in range(REM_HI):
            r = (LOCAL_HI + h) * GROUP
            rem_ref[at, h * LO : (h + 1) * LO] = counts[r : r + GROUP, :]
        return carry

    lax.fori_loop(0, TILE // GROUP, build, 0, unroll=2)
    agg_ref[...] = jnp.dot(loc_ref[...], xall_ref[...], preferred_element_type=F32)
    x = x_ref[...]
    base_ref[...] = jnp.dot(x, wself_ref[...], preferred_element_type=F32)
    hidden = jnp.maximum(jnp.dot(x, sfirst_ref[...], preferred_element_type=F32), 0.0).astype(BF)
    sh_ref[...] = hidden
    logits = jnp.dot(hidden, ssecond_ref[...], preferred_element_type=F32)
    ps_ref[...] = soft(logits)


def soft(logits):
    scaled = logits / TEMPER
    e = jnp.exp(scaled - jnp.max(scaled, axis=-1, keepdims=True))
    return e / jnp.sum(e, axis=-1, keepdims=True)


def whole(shape):
    return pl.BlockSpec(shape, lambda i: (0,) * len(shape), pipeline_mode=pl.Buffered(1))


def local_part(idx, feats, w_self, s_first, s_second):
    rem = REM_HI * LO
    tile = lambda n: pl.BlockSpec((TILE, n), lambda i: (i, 0))
    return pl.pallas_call(
        local_kernel,
        grid=(ROWS // TILE,),
        in_specs=[
            pl.BlockSpec((TILE // GROUP, LO), lambda i: (i, 0)),
            tile(WIDTH), whole((ROWS, WIDTH)), whole((WIDTH, WIDTH)), whole((WIDTH, WIDTH)), whole((WIDTH, 128)),
        ],
        out_specs=[tile(WIDTH), tile(rem), tile(WIDTH), tile(WIDTH), tile(128)],
        out_shape=[
            jax.ShapeDtypeStruct((ROWS, WIDTH), F32),
            jax.ShapeDtypeStruct((ROWS, rem), BF),
            jax.ShapeDtypeStruct((ROWS, WIDTH), F32),
            jax.ShapeDtypeStruct((ROWS, WIDTH), BF),
            jax.ShapeDtypeStruct((ROWS, 128), F32),
        ],
        scratch_shapes=[pltpu.VMEM((TILE, ROWS), BF)],
        compiler_params=pltpu.CompilerParams(
            dimension_semantics=("arbitrary",), vmem_limit_bytes=56 << 20
        ),
        cost_estimate=pl.CostEstimate(flops=25_000_000_000, bytes_accessed=30_000_000, transcendentals=0),
        name="local_part",
    )(idx, feats, feats, w_self, s_first, s_second)


def tail_kernel(
    scale, agg_ref, rem_ref, base_ref, sh_ref, ps_ref, x_ref, r_ref, p1, p2, p3, p4, p5, p6, p7,
    wneigh_ref, whead_ref, ssecond_ref, hid_ref, g_ref,
):
    @pl.when(pl.program_id(0) == 0)
    def _():
        g_ref[...] = jnp.zeros_like(g_ref)

    first = PEERS * SLOT
    acc = agg_ref[...] + jnp.dot(rem_ref[:, 0:first], r_ref[...], preferred_element_type=F32)
    for n, part in enumerate((p1, p2, p3, p4, p5, p6, p7)):
        at = first + n * LO
        acc = acc + jnp.dot(rem_ref[:, at : at + LO], part[...], preferred_element_type=F32)
    agg = (acc / DEG).astype(BF)
    pre = base_ref[...] + jnp.dot(agg, wneigh_ref[...], preferred_element_type=F32)
    hidden = jnp.maximum(pre, 0.0).astype(BF)
    hid_ref[...] = hidden
    teach = soft(jnp.dot(hidden, whead_ref[...], preferred_element_type=F32))
    delta = (TEMPER * (ps_ref[...] - teach) * scale).astype(BF)
    sh = sh_ref[...]
    back = lax.dot_general(delta, ssecond_ref[...], NT, preferred_element_type=F32)
    back = jnp.where(sh.astype(F32) > 0.0, back, 0.0).astype(BF)
    first_grad = lax.dot_general(x_ref[...], back, TN, preferred_element_type=F32)
    for c in range(4):
        g_ref[c * WIDTH : (c + 1) * WIDTH, :] += first_grad[:, c * 128 : (c + 1) * 128]
    g_ref[4 * WIDTH : 5 * WIDTH, :] += lax.dot_general(sh, delta, TN, preferred_element_type=F32)


def tail_part(scale, agg, rem, base, sh, ps, feats, got, parts, w_neigh, w_head, s_second):
    tile = lambda n: pl.BlockSpec((TILE, n), lambda i: (i, 0))
    return pl.pallas_call(
        functools.partial(tail_kernel, scale),
        grid=(ROWS // TILE,),
        in_specs=[
            tile(WIDTH), tile(REM_HI * LO), tile(WIDTH), tile(WIDTH), tile(128), tile(WIDTH),
            whole((PEERS * SLOT, WIDTH)),
        ]
        + [whole((LO, WIDTH))] * 7
        + [whole((WIDTH, WIDTH)), whole((WIDTH, 128)), whole((WIDTH, 128))],
        out_specs=[tile(WIDTH), pl.BlockSpec((5 * WIDTH, 128), lambda i: (0, 0))],
        out_shape=[
            jax.ShapeDtypeStruct((ROWS, WIDTH), BF),
            jax.ShapeDtypeStruct((5 * WIDTH, 128), F32),
        ],
        compiler_params=pltpu.CompilerParams(
            dimension_semantics=("arbitrary",), vmem_limit_bytes=56 << 20
        ),
        cost_estimate=pl.CostEstimate(flops=10_000_000_000, bytes_accessed=30_000_000, transcendentals=0),
        name="tail_part",
    )(agg, rem, base, sh, ps, feats, got, *parts, w_neigh, w_head, s_second)


def remap(neighbours, y, c):
    idx = neighbours
    halo = idx - ROWS
    halo_at = (halo // CAP) * SLOT + halo % CAP
    hub = idx - ROWS - PEERS * CAP
    block = hub // LO
    inner = hub % LO
    shift = (y - block // 2) % NY
    cross = (block % 2) ^ c
    own_at = (inner // HUBD) * SLOT + CAP + inner % HUBD
    other = cross * NY + shift
    far_at = PEERS * SLOT + (other - 1) * LO + inner
    hub_at = jnp.where(other == 0, own_at, far_at)
    out = jnp.where(idx < ROWS, idx, ROWS + jnp.where(idx < ROWS + PEERS * CAP, halo_at, hub_at))
    return out.reshape(ROWS // GROUP, GROUP * DEG)


def a2a(x, axes):
    return lax.all_to_all(x, axes, split_axis=0, concat_axis=0, tiled=True)


def copies(x, n):
    return jnp.broadcast_to(x[None], (n,) + x.shape).reshape((n * x.shape[0],) + x.shape[1:])


def per_device(feats, send_rows, hub_rows, neighbours, w_self, w_neigh, w_head, s_first, s_second):
    y = lax.axis_index("y")
    c = lax.axis_index("core")
    total = ROWS * NY * NC * NZ * NX
    scale = 1.0 / float(total) ** 0.5

    out = send_rows_of(feats, send_rows[0], hub_rows)
    got = a2a(out, DOM)
    idx = remap(neighbours, y, c)
    agg, rem, base, sh, ps = local_part(idx, feats, w_self, s_first, s_second)
    own = got[:, CAP:SLOT, :].reshape(LO, WIDTH)
    ring = [own] + [
        lax.ppermute(own, "y", [(i, (i + k) % NY) for i in range(NY)]) for k in range(1, NY)
    ]
    swap = [lax.ppermute(r, "core", [(0, 1), (1, 0)]) for r in ring]
    hidden, g = tail_part(
        scale, agg, rem, base, sh, ps, feats, got.reshape(PEERS * SLOT, WIDTH), ring[1:] + swap,
        w_neigh, w_head, s_second,
    )
    n1 = NY * NC * NX
    piece = 5 * WIDTH // n1
    part = jnp.sum(a2a(g, YCX).reshape(n1, piece, 128), axis=0)
    part = jnp.sum(a2a(copies(part, NZ), "z").reshape(NZ, piece, 128), axis=0)
    g = a2a(copies(part, n1), YCX).reshape(5, WIDTH, 128)
    grad_first = g[:4].transpose(1, 0, 2).reshape(WIDTH, WIDTH)
    return hidden, grad_first, g[4]


def solution(mesh):
    inner = Mesh(mesh.devices.reshape(NY, NC, NZ, NX), ALL)
    return jax.shard_map(
        per_device,
        mesh=inner,
        in_specs=(P(ALL, None), P(ALL, None, None), P(ALL, None), P(ALL, None), P(), P(), P(), P(), P()),
        out_specs=(P(ALL, None), P(), P()),
        check_vma=False,
    )
```

```python
import functools

import jax
import jax.numpy as jnp
from jax import lax
from jax.experimental import pallas as pl
from jax.experimental.pallas import tpu as pltpu
from jax.sharding import Mesh
from jax.sharding import PartitionSpec as P

DEG = 16
TEMPER = 2.0
NY, NC, NZ, NX = 4, 2, 8, 4
ALL = ("y", "core", "z", "x")
DOM = ("z", "x")
PLANE = ("y", "x")
BF = jnp.bfloat16
F32 = jnp.float32
LAST = jnp.float32
NT = (((1,), (1,)), ((), ()))
TN = (((0,), (0,)), ((), ()))

ROWS = 2048
WIDTH = 512
PEERS = 32
CAP = 32
HUBD = 8
SLOT = CAP + HUBD
LO = 256
LOCAL_HI = ROWS // LO
REM_HI = 12
GROUP = 16
TILE = 512
VMEM = 60 << 20
UNROLL = 2


def onehot(cond):
    return jnp.where(cond, 1.0, 0.0).astype(BF)


def params():
    return pltpu.CompilerParams(dimension_semantics=("arbitrary",), vmem_limit_bytes=VMEM)


def plain():
    return pltpu.CompilerParams(vmem_limit_bytes=VMEM)


def pick_kernel(rows_ref, hub_ref, x_ref, out_ref):
    x = x_ref[...]
    rows_t = rows_ref[...].T
    lane = lax.broadcasted_iota(jnp.int32, (CAP, ROWS), 1)
    per = 8
    hub_t = hub_ref[...].T
    hub_lane = lax.broadcasted_iota(jnp.int32, (HUBD, ROWS), 1)
    hubs = jnp.dot(onehot(hub_t[:, 0:1] == hub_lane), x, preferred_element_type=F32).astype(BF)
    for block in range(PEERS // per):
        picks = jnp.concatenate(
            [onehot(rows_t[:, s : s + 1] == lane) for s in range(block * per, (block + 1) * per)], axis=0
        )
        got = jnp.dot(picks, x, preferred_element_type=F32).astype(BF)
        for n in range(per):
            out_ref[block * per + n, 0:CAP, :] = got[n * CAP : (n + 1) * CAP, :]
            out_ref[block * per + n, CAP:SLOT, :] = hubs


def pick_rows(feats, send_rows, hub_rows):
    return pl.pallas_call(
        pick_kernel,
        out_shape=jax.ShapeDtypeStruct((PEERS, SLOT, WIDTH), BF),
        compiler_params=plain(),
        cost_estimate=pl.CostEstimate(flops=3_000_000_000, bytes_accessed=3_000_000, transcendentals=0),
        name="pick_rows",
    )(send_rows, hub_rows, feats)


def count_kernel(idx_ref, xall_ref, agg_ref, rem_ref, loc_ref):
    high = (LOCAL_HI + REM_HI) * GROUP
    left_row = lax.broadcasted_iota(jnp.int32, (high, LO), 0)
    low_row = lax.broadcasted_iota(jnp.int32, (LO, LO), 0)
    node = lax.broadcasted_iota(jnp.int32, (1, LO), 1) // DEG

    def build(g, carry):
        idx = idx_ref[pl.ds(g, 1), :]
        where_hi = (idx // LO) * GROUP + node
        where_lo = idx % LO
        left = onehot(jnp.broadcast_to(where_hi, (high, LO)) == left_row)
        low = onehot(jnp.broadcast_to(where_lo, (LO, LO)) == low_row)
        counts = lax.dot_general(left, low, NT, preferred_element_type=F32).astype(BF)
        at = pl.ds(pl.multiple_of(g * GROUP, GROUP), GROUP)
        for h in range(LOCAL_HI):
            loc_ref[at, h * LO : (h + 1) * LO] = counts[h * GROUP : (h + 1) * GROUP, :]
        for h in range(REM_HI):
            r = (LOCAL_HI + h) * GROUP
            rem_ref[at, h * LO : (h + 1) * LO] = counts[r : r + GROUP, :]
        return carry

    lax.fori_loop(0, TILE // GROUP, build, 0, unroll=UNROLL)
    agg_ref[...] = jnp.dot(loc_ref[...], xall_ref[...], preferred_element_type=F32)


def count_part(idx, feats):
    rem = REM_HI * LO
    return pl.pallas_call(
        count_kernel,
        grid=(ROWS // TILE,),
        in_specs=[pl.BlockSpec((TILE // GROUP, LO), lambda i: (i, 0)), whole((ROWS, WIDTH))],
        out_specs=[tile(WIDTH), tile(rem)],
        out_shape=[jax.ShapeDtypeStruct((ROWS, WIDTH), F32), jax.ShapeDtypeStruct((ROWS, rem), BF)],
        scratch_shapes=[pltpu.VMEM((TILE, ROWS), BF)],
        compiler_params=params(),
        cost_estimate=pl.CostEstimate(flops=25_000_000_000, bytes_accessed=20_000_000, transcendentals=0),
        name="count_part",
    )(idx, feats)


def soft(logits):
    scaled = logits / TEMPER
    e = jnp.exp(scaled - jnp.max(scaled, axis=-1, keepdims=True))
    return e / jnp.sum(e, axis=-1, keepdims=True)


def dense_kernel(x_ref, wself_ref, sfirst_ref, ssecond_ref, base_ref, sh_ref, ps_ref):
    x = x_ref[...]
    base_ref[...] = jnp.dot(x, wself_ref[...], preferred_element_type=F32)
    hidden = jnp.maximum(jnp.dot(x, sfirst_ref[...], preferred_element_type=F32), 0.0).astype(BF)
    sh_ref[...] = hidden
    ps_ref[...] = soft(jnp.dot(hidden, ssecond_ref[...], preferred_element_type=F32))


def whole(shape):
    return pl.BlockSpec(shape, lambda i: (0,) * len(shape), pipeline_mode=pl.Buffered(1))


def tile(n):
    return pl.BlockSpec((TILE, n), lambda i: (i, 0))


def dense_part(feats, w_self, s_first, s_second):
    return pl.pallas_call(
        dense_kernel,
        grid=(ROWS // TILE,),
        in_specs=[tile(WIDTH), whole((WIDTH, WIDTH)), whole((WIDTH, WIDTH)), whole((WIDTH, 128))],
        out_specs=[tile(WIDTH), tile(WIDTH), tile(128)],
        out_shape=[
            jax.ShapeDtypeStruct((ROWS, WIDTH), F32),
            jax.ShapeDtypeStruct((ROWS, WIDTH), BF),
            jax.ShapeDtypeStruct((ROWS, 128), F32),
        ],
        compiler_params=params(),
        cost_estimate=pl.CostEstimate(flops=3_000_000_000, bytes_accessed=10_000_000, transcendentals=0),
        name="dense_part",
    )(feats, w_self, s_first, s_second)


def tail_kernel(
    scale, pos_ref, agg_ref, rem_ref, base_ref, sh_ref, ps_ref, x_ref, r_ref, p1, p2, p3, p4, p5, p6, p7,
    wneigh_ref, whead_ref, ssecond_ref, hid_ref, keep_ref, send_ref, g_ref,
):
    step = pl.program_id(0)

    @pl.when(step == 0)
    def _():
        g_ref[...] = jnp.zeros_like(g_ref)

    first = PEERS * SLOT
    acc = agg_ref[...] + jnp.dot(rem_ref[:, 0:first], r_ref[...], preferred_element_type=F32)
    for n, part in enumerate((p1, p2, p3, p4, p5, p6, p7)):
        at = first + n * LO
        acc = acc + jnp.dot(rem_ref[:, at : at + LO], part[...], preferred_element_type=F32)
    agg = (acc / DEG).astype(BF)
    pre = base_ref[...] + jnp.dot(agg, wneigh_ref[...], preferred_element_type=F32)
    hidden = jnp.maximum(pre, 0.0).astype(BF)
    hid_ref[...] = hidden
    teach = soft(jnp.dot(hidden, whead_ref[...], preferred_element_type=F32))
    delta = (TEMPER * (ps_ref[...] - teach) * scale).astype(BF)
    sh = sh_ref[...]
    back = lax.dot_general(delta, ssecond_ref[...], NT, preferred_element_type=F32)
    back = jnp.where(sh.astype(F32) > 0.0, back, 0.0).astype(BF)
    first_grad = lax.dot_general(x_ref[...], back, TN, preferred_element_type=F32)
    for c in range(4):
        g_ref[c * WIDTH : (c + 1) * WIDTH, :] += first_grad[:, c * 128 : (c + 1) * 128]
    g_ref[4 * WIDTH : 5 * WIDTH, :] += lax.dot_general(sh, delta, TN, preferred_element_type=F32)

    @pl.when(step == pl.num_programs(0) - 1)
    def _():
        core = pos_ref[1]
        keep_ref[...] = g_ref[pl.ds(pl.multiple_of(core * HALF, 8), HALF), :]
        send_ref[...] = g_ref[pl.ds(pl.multiple_of((1 - core) * HALF, 8), HALF), :]


SMEM_SPEC = pl.BlockSpec(memory_space=pltpu.SMEM)


def tail_part(scale, pos, agg, rem, base, sh, ps, feats, got, parts, w_neigh, w_head, s_second):
    fixed = pl.BlockSpec((HALF, 128), lambda i: (0, 0))
    return pl.pallas_call(
        functools.partial(tail_kernel, scale),
        grid=(ROWS // TILE,),
        in_specs=[
            SMEM_SPEC, tile(WIDTH), tile(REM_HI * LO), tile(WIDTH), tile(WIDTH), tile(128), tile(WIDTH),
            whole((PEERS * SLOT, WIDTH)),
        ]
        + [whole((LO, WIDTH))] * 7
        + [whole((WIDTH, WIDTH)), whole((WIDTH, 128)), whole((WIDTH, 128))],
        out_specs=[tile(WIDTH), fixed, fixed],
        out_shape=[
            jax.ShapeDtypeStruct((ROWS, WIDTH), BF),
            jax.ShapeDtypeStruct((HALF, 128), F32),
            jax.ShapeDtypeStruct((HALF, 128), F32),
        ],
        scratch_shapes=[pltpu.VMEM((2 * HALF, 128), F32)],
        compiler_params=params(),
        cost_estimate=pl.CostEstimate(flops=10_000_000_000, bytes_accessed=30_000_000, transcendentals=0),
        name="tail_part",
    )(pos, agg, rem, base, sh, ps, feats, got, *parts, w_neigh, w_head, s_second)


HALF = 5 * WIDTH // 2


def unpack_kernel(pos_ref, mine_ref, other_ref, first, second, g_ref):
    core = pos_ref[1]
    g_ref[pl.ds(pl.multiple_of(core * HALF, 16), HALF), :] = mine_ref[...].astype(F32)
    g_ref[pl.ds(pl.multiple_of((1 - core) * HALF, 16), HALF), :] = other_ref[...].astype(F32)
    for c in range(4):
        first[:, c * 128 : (c + 1) * 128] = g_ref[c * WIDTH : (c + 1) * WIDTH, :]
    second[...] = g_ref[4 * WIDTH : 5 * WIDTH, :]


def unpack(pos, mine, other):
    vmem = pl.BlockSpec(memory_space=pltpu.VMEM)
    return pl.pallas_call(
        unpack_kernel,
        in_specs=[SMEM_SPEC, vmem, vmem],
        out_specs=[vmem, vmem],
        out_shape=[jax.ShapeDtypeStruct((WIDTH, WIDTH), F32), jax.ShapeDtypeStruct((WIDTH, 128), F32)],
        scratch_shapes=[pltpu.VMEM((2 * HALF, 128), F32)],
        compiler_params=pltpu.CompilerParams(vmem_limit_bytes=16 << 20),
        name="unpack",
    )(pos, mine, other)


def shift(x, axis, n, k):
    return lax.ppermute(x, axis, [(i, (i + k) % n) for i in range(n)])


def swap(x):
    return lax.ppermute(x, "core", [(0, 1), (1, 0)])


def reduce_grads(pos, keep, send):
    total = keep + swap(send)
    plane = NY * NX
    piece = HALF // plane
    part = jnp.sum(a2a(total, PLANE).reshape(plane, piece, 128), axis=0)
    part = jnp.sum(a2a(copies(part, NZ), "z").reshape(NZ, piece, 128), axis=0)
    mine = a2a(copies(part.astype(LAST), plane), PLANE)
    return unpack(pos, mine, swap(mine))


def remap(neighbours, y, c):
    halo = neighbours - ROWS
    halo_at = ROWS + (halo // CAP) * SLOT + halo % CAP
    hub = halo - PEERS * CAP
    inner = hub % LO
    block = hub // LO
    other = ((block % 2) ^ c) * NY + (y - block // 2) % NY
    own_at = ROWS + (inner // HUBD) * SLOT + CAP + inner % HUBD
    far_at = ROWS + PEERS * SLOT + (other - 1) * LO + inner
    hub_at = jnp.where(other == 0, own_at, far_at)
    out = jnp.where(halo < 0, neighbours, jnp.where(hub < 0, halo_at, hub_at))
    return out.reshape(ROWS // GROUP, GROUP * DEG)


def a2a(x, axes):
    return lax.all_to_all(x, axes, split_axis=0, concat_axis=0, tiled=True)


def copies(x, n):
    return jnp.broadcast_to(x[None], (n,) + x.shape).reshape((n * x.shape[0],) + x.shape[1:])


def body(feats, send_rows, hub_rows, neighbours, w_self, w_neigh, w_head, s_first, s_second):
    y = lax.axis_index("y")
    c = lax.axis_index("core")
    pos = jnp.stack([y, c, lax.axis_index("z"), lax.axis_index("x")]).astype(jnp.int32)
    scale = 1.0 / float(ROWS * NY * NC * NZ * NX) ** 0.5

    out = pick_rows(feats, send_rows[0], hub_rows)
    idx = remap(neighbours, y, c)
    got = a2a(out, DOM)
    agg, rem = count_part(idx, feats)
    own = got[:, CAP:SLOT, :].reshape(LO, WIDTH)
    ring = [own] + [shift(own, "y", NY, k) for k in range(1, NY)]
    base, sh, ps = dense_part(feats, w_self, s_first, s_second)
    cross = [swap(r) for r in ring]
    hidden, keep, send = tail_part(
        scale, pos, agg, rem, base, sh, ps, feats, got.reshape(PEERS * SLOT, WIDTH), ring[1:] + cross,
        w_neigh, w_head, s_second,
    )
    grad_first, grad_second = reduce_grads(pos, keep, send)
    return hidden, grad_first, grad_second


def solution(mesh):
    inner = Mesh(mesh.devices.reshape(NY, NC, NZ, NX), ALL)
    return jax.shard_map(
        body,
        mesh=inner,
        in_specs=(P(ALL, None), P(ALL, None, None), P(ALL, None), P(ALL, None), P(), P(), P(), P(), P()),
        out_specs=(P(ALL, None), P(), P()),
        check_vma=False,
    )
```

```python
import functools

import jax
import jax.numpy as jnp
from jax import lax
from jax.experimental import pallas as pl
from jax.experimental.pallas import tpu as pltpu
from jax.sharding import Mesh
from jax.sharding import PartitionSpec as P

DEG = 16
TEMPER = 2.0
NY, NC, NZ, NX = 4, 2, 8, 4
ALL = ("y", "core", "z", "x")
DOM = ("z", "x")
PLANE = ("y", "x")
BF = jnp.bfloat16
F32 = jnp.float32
LAST = jnp.float32
NT = (((1,), (1,)), ((), ()))
TN = (((0,), (0,)), ((), ()))

ROWS = 2048
WIDTH = 512
PEERS = 32
CAP = 32
HUBD = 8
LO = 256
LOCAL_HI = ROWS // LO
REM_HI = 12
GROUP = 16
TILE = 512
VMEM = 30 << 20
UNROLL = 16
FIRST = 1


def onehot(cond):
    return jnp.where(cond, 1.0, 0.0).astype(BF)


def params():
    return pltpu.CompilerParams(dimension_semantics=("arbitrary",), vmem_limit_bytes=VMEM)


def plain():
    return pltpu.CompilerParams(vmem_limit_bytes=VMEM)


def hub_kernel(hub_ref, x_ref, out_ref):
    hub_t = hub_ref[...].T
    lane = lax.broadcasted_iota(jnp.int32, (HUBD, ROWS), 1)
    hubs = jnp.dot(onehot(hub_t[:, 0:1] == lane), x_ref[...], preferred_element_type=F32).astype(BF)
    for s in range(PEERS):
        out_ref[s] = hubs


def halo_kernel(rows_ref, x_ref, out_ref):
    x = x_ref[...]
    rows_t = rows_ref[...].T
    lane = lax.broadcasted_iota(jnp.int32, (CAP, ROWS), 1)
    per = 8
    for block in range(PEERS // per):
        picks = jnp.concatenate(
            [onehot(rows_t[:, s : s + 1] == lane) for s in range(block * per, (block + 1) * per)], axis=0
        )
        got = jnp.dot(picks, x, preferred_element_type=F32).astype(BF)
        for n in range(per):
            out_ref[block * per + n] = got[n * CAP : (n + 1) * CAP, :]


def hub_rows_of(feats, hub_rows):
    return pl.pallas_call(
        hub_kernel,
        out_shape=pltpu.HBM((PEERS, HUBD, WIDTH), BF),
        compiler_params=plain(),
        name="hub_rows",
    )(hub_rows, feats)


def halo_rows_of(feats, send_rows):
    return pl.pallas_call(
        halo_kernel,
        out_shape=pltpu.HBM((PEERS, CAP, WIDTH), BF),
        compiler_params=plain(),
        cost_estimate=pl.CostEstimate(flops=3_000_000_000, bytes_accessed=3_000_000, transcendentals=0),
        name="halo_rows",
    )(send_rows, feats)


def count_kernel(idx_ref, xall_ref, *refs):
    agg_ref, rem_ref, loc_ref = refs[-3:]
    high = (LOCAL_HI + REM_HI) * GROUP
    left_row = lax.broadcasted_iota(jnp.int32, (high, LO), 0)
    low_row = lax.broadcasted_iota(jnp.int32, (LO, LO), 0)
    node = lax.broadcasted_iota(jnp.int32, (1, LO), 1) // DEG

    def build(g, carry):
        idx = idx_ref[pl.ds(g, 1), :]
        where_hi = (idx >> 8) * GROUP + node
        where_lo = idx & (LO - 1)
        left = onehot(jnp.broadcast_to(where_hi, (high, LO)) == left_row)
        low = onehot(jnp.broadcast_to(where_lo, (LO, LO)) == low_row)
        counts = lax.dot_general(left, low, NT, preferred_element_type=F32).astype(BF)
        at = pl.ds(pl.multiple_of(g * GROUP, GROUP), GROUP)
        for h in range(LOCAL_HI):
            loc_ref[at, h * LO : (h + 1) * LO] = counts[h * GROUP : (h + 1) * GROUP, :]
        for h in range(REM_HI):
            r = (LOCAL_HI + h) * GROUP
            rem_ref[at, h * LO : (h + 1) * LO] = counts[r : r + GROUP, :]
        return carry

    lax.fori_loop(0, TILE // GROUP, build, 0, unroll=UNROLL)
    agg_ref[...] = jnp.dot(loc_ref[...], xall_ref[...], preferred_element_type=F32)


def count_part(idx, feats, at, steps, before):
    rem = REM_HI * LO
    rows = lambda n: pl.BlockSpec((TILE, n), lambda i: (i + at, 0))
    return pl.pallas_call(
        count_kernel,
        grid=(steps,),
        in_specs=[pl.BlockSpec((TILE // GROUP, LO), lambda i: (i + at, 0)), whole()]
        + [pl.BlockSpec(memory_space=pl.ANY)] * len(before),
        out_specs=[rows(WIDTH), rows(rem)],
        out_shape=[pltpu.HBM((ROWS, WIDTH), F32), pltpu.HBM((ROWS, rem), BF)],
        scratch_shapes=[pltpu.VMEM((TILE, ROWS), BF)],
        input_output_aliases={2: 0, 3: 1} if before else {},
        compiler_params=params(),
        cost_estimate=pl.CostEstimate(
            flops=5_000_000_000 * steps, bytes_accessed=5_000_000 * steps, transcendentals=0
        ),
        name="count_part",
    )(idx, feats, *before)


def soft(logits):
    scaled = logits / TEMPER
    e = jnp.exp(scaled - jnp.max(scaled, axis=-1, keepdims=True))
    return e / jnp.sum(e, axis=-1, keepdims=True)


def dense_kernel(x_ref, wself_ref, sfirst_ref, ssecond_ref, base_ref, sh_ref, ps_ref):
    x = x_ref[...]
    base_ref[...] = jnp.dot(x, wself_ref[...], preferred_element_type=F32)
    hidden = jnp.maximum(jnp.dot(x, sfirst_ref[...], preferred_element_type=F32), 0.0).astype(BF)
    sh_ref[...] = hidden
    ps_ref[...] = soft(jnp.dot(hidden, ssecond_ref[...], preferred_element_type=F32))


def whole():
    return pl.BlockSpec(memory_space=pltpu.VMEM)


def once(shape):
    return pl.BlockSpec(shape, lambda i: (0,) * len(shape), pipeline_mode=pl.Buffered(1))


def hbm(x):
    return pltpu.with_memory_space_constraint(x, pltpu.HBM)


def tile(n):
    return pl.BlockSpec((TILE, n), lambda i: (i, 0))


def dense_part(feats, w_self, s_first, s_second):
    return pl.pallas_call(
        dense_kernel,
        grid=(ROWS // TILE,),
        in_specs=[tile(WIDTH), whole(), whole(), whole()],
        out_specs=[tile(WIDTH), tile(WIDTH), tile(128)],
        out_shape=[pltpu.HBM((ROWS, WIDTH), F32), pltpu.HBM((ROWS, WIDTH), BF), pltpu.HBM((ROWS, 128), F32)],
        compiler_params=params(),
        cost_estimate=pl.CostEstimate(flops=3_000_000_000, bytes_accessed=10_000_000, transcendentals=0),
        name="dense_part",
    )(hbm(feats), w_self, s_first, s_second)


def tail_kernel(
    scale, pos_ref, agg_ref, rem_ref, base_ref, sh_ref, ps_ref, x_ref, r_ref, p0, p1, p2, p3, p4, p5, p6, p7,
    wneigh_ref, whead_ref, ssecond_ref, hid_ref, keep_ref, send_ref, g_ref,
):
    step = pl.program_id(0)

    @pl.when(step == 0)
    def _():
        g_ref[...] = jnp.zeros_like(g_ref)

    first = PEERS * CAP
    acc = agg_ref[...] + jnp.dot(rem_ref[:, 0:first], r_ref[...], preferred_element_type=F32)
    for n, part in enumerate((p0, p1, p2, p3, p4, p5, p6, p7)):
        at = first + n * LO
        acc = acc + jnp.dot(rem_ref[:, at : at + LO], part[...], preferred_element_type=F32)
    agg = (acc / DEG).astype(BF)
    pre = base_ref[...] + jnp.dot(agg, wneigh_ref[...], preferred_element_type=F32)
    hidden = jnp.maximum(pre, 0.0).astype(BF)
    hid_ref[...] = hidden
    teach = soft(jnp.dot(hidden, whead_ref[...], preferred_element_type=F32))
    delta = (TEMPER * (ps_ref[...] - teach) * scale).astype(BF)
    sh = sh_ref[...]
    back = lax.dot_general(delta, ssecond_ref[...], NT, preferred_element_type=F32)
    back = jnp.where(sh.astype(F32) > 0.0, back, 0.0).astype(BF)
    first_grad = lax.dot_general(x_ref[...], back, TN, preferred_element_type=F32)
    for c in range(4):
        g_ref[c * WIDTH : (c + 1) * WIDTH, :] += first_grad[:, c * 128 : (c + 1) * 128]
    g_ref[4 * WIDTH : 5 * WIDTH, :] += lax.dot_general(sh, delta, TN, preferred_element_type=F32)

    @pl.when(step == pl.num_programs(0) - 1)
    def _():
        core = pos_ref[1]
        keep_ref[...] = g_ref[pl.ds(pl.multiple_of(core * HALF, 8), HALF), :]
        send_ref[...] = g_ref[pl.ds(pl.multiple_of((1 - core) * HALF, 8), HALF), :]


SMEM_SPEC = pl.BlockSpec(memory_space=pltpu.SMEM)


def tail_part(scale, pos, agg, rem, base, sh, ps, feats, got, parts, w_neigh, w_head, s_second):
    fixed = pl.BlockSpec((HALF, 128), lambda i: (0, 0))
    return pl.pallas_call(
        functools.partial(tail_kernel, scale),
        grid=(ROWS // TILE,),
        in_specs=[
            SMEM_SPEC, tile(WIDTH), tile(REM_HI * LO), tile(WIDTH), tile(WIDTH), tile(128), tile(WIDTH),
            once((PEERS * CAP, WIDTH)),
        ]
        + [once((LO, WIDTH))] * 8
        + [whole(), whole(), whole()],
        out_specs=[tile(WIDTH), fixed, fixed],
        out_shape=[
            pltpu.HBM((ROWS, WIDTH), BF),
            jax.ShapeDtypeStruct((HALF, 128), F32),
            jax.ShapeDtypeStruct((HALF, 128), F32),
        ],
        scratch_shapes=[pltpu.VMEM((2 * HALF, 128), F32)],
        compiler_params=params(),
        cost_estimate=pl.CostEstimate(flops=10_000_000_000, bytes_accessed=30_000_000, transcendentals=0),
        name="tail_part",
    )(pos, *map(hbm, (agg, rem, base, sh, ps, feats, got, *parts)), w_neigh, w_head, s_second)


HALF = 5 * WIDTH // 2


def unpack_kernel(pos_ref, mine_ref, other_ref, first, second, g_ref):
    core = pos_ref[1]
    g_ref[pl.ds(pl.multiple_of(core * HALF, 16), HALF), :] = mine_ref[...].astype(F32)
    g_ref[pl.ds(pl.multiple_of((1 - core) * HALF, 16), HALF), :] = other_ref[...].astype(F32)
    for c in range(4):
        first[:, c * 128 : (c + 1) * 128] = g_ref[c * WIDTH : (c + 1) * WIDTH, :]
    second[...] = g_ref[4 * WIDTH : 5 * WIDTH, :]


def unpack(pos, mine, other):
    vmem = pl.BlockSpec(memory_space=pltpu.VMEM)
    return pl.pallas_call(
        unpack_kernel,
        in_specs=[SMEM_SPEC, vmem, vmem],
        out_specs=[vmem, vmem],
        out_shape=[jax.ShapeDtypeStruct((WIDTH, WIDTH), F32), jax.ShapeDtypeStruct((WIDTH, 128), F32)],
        scratch_shapes=[pltpu.VMEM((2 * HALF, 128), F32)],
        compiler_params=pltpu.CompilerParams(vmem_limit_bytes=16 << 20),
        name="unpack",
    )(pos, mine, other)


def shift(x, axis, n, k):
    return lax.ppermute(x, axis, [(i, (i + k) % n) for i in range(n)])


def swap(x):
    return lax.ppermute(x, "core", [(0, 1), (1, 0)])


def reduce_grads(pos, keep, send):
    total = keep + swap(send)
    plane = NY * NX
    piece = HALF // plane
    part = jnp.sum(a2a(total, PLANE).reshape(plane, piece, 128), axis=0)
    part = jnp.sum(a2a(copies(part, NZ), "z").reshape(NZ, piece, 128), axis=0)
    mine = a2a(copies(part.astype(LAST), plane), PLANE)
    return unpack(pos, mine, swap(mine))


def remap(neighbours, y, c):
    hub = neighbours - ROWS - PEERS * CAP
    block = hub // LO
    other = ((block % 2) ^ c) * NY + (y - block // 2) % NY
    far = ROWS + PEERS * CAP + other * LO + hub % LO
    out = jnp.where(hub < 0, neighbours, far)
    return out.reshape(ROWS // GROUP, GROUP * DEG)


def a2a(x, axes):
    return lax.all_to_all(x, axes, split_axis=0, concat_axis=0, tiled=True)


def copies(x, n):
    return jnp.broadcast_to(x[None], (n,) + x.shape).reshape((n * x.shape[0],) + x.shape[1:])


def body(feats, send_rows, hub_rows, neighbours, w_self, w_neigh, w_head, s_first, s_second):
    y = lax.axis_index("y")
    c = lax.axis_index("core")
    pos = jnp.stack([y, c, lax.axis_index("z"), lax.axis_index("x")]).astype(jnp.int32)
    scale = 1.0 / float(ROWS * NY * NC * NZ * NX) ** 0.5

    own = a2a(hub_rows_of(feats, hub_rows), DOM).reshape(LO, WIDTH)
    out = halo_rows_of(feats, send_rows[0])
    idx = remap(neighbours, y, c)
    counts = count_part(idx, feats, 0, FIRST, [])
    got = a2a(out, DOM)
    ring = [own] + [shift(own, "y", NY, k) for k in range(1, NY)]
    agg, rem = count_part(idx, feats, FIRST, ROWS // TILE - FIRST, counts)
    cross = [swap(r) for r in ring]
    base, sh, ps = dense_part(feats, w_self, s_first, s_second)
    hidden, keep, send = tail_part(
        scale, pos, agg, rem, base, sh, ps, feats, got.reshape(PEERS * CAP, WIDTH), ring + cross,
        w_neigh, w_head, s_second,
    )
    grad_first, grad_second = reduce_grads(pos, keep, send)
    return hidden, grad_first, grad_second


def solution(mesh):
    inner = Mesh(mesh.devices.reshape(NY, NC, NZ, NX), ALL)
    return jax.shard_map(
        body,
        mesh=inner,
        in_specs=(P(ALL, None), P(ALL, None, None), P(ALL, None), P(ALL, None), P(), P(), P(), P(), P()),
        out_specs=(P(ALL, None), P(), P()),
        check_vma=False,
    )
```

```python
import functools

import jax
import jax.numpy as jnp
from jax import lax
from jax.experimental import pallas as pl
from jax.experimental.pallas import tpu as pltpu
from jax.sharding import Mesh
from jax.sharding import PartitionSpec as P

DEG = 16
TEMPER = 2.0
NY, NC, NZ, NP, NX = 4, 2, 4, 2, 4
ALL = ("y", "core", "z", "pair", "x")
DOM = ("z", "pair", "x")
PLANE = ("y", "pair", "x")
BF = jnp.bfloat16
F32 = jnp.float32
LAST = jnp.float32
NT = (((1,), (1,)), ((), ()))
TN = (((0,), (0,)), ((), ()))

ROWS = 2048
WIDTH = 512
PEERS = 32
CAP = 32
HUBD = 8
LO = 256
LOCAL_HI = ROWS // LO
REM_HI = 12
FAR = 4
GROUP = 16
TILE = 512
VMEM = 30 << 20
UNROLL = 16
FIRST = 1


def onehot(cond):
    return jnp.where(cond, 1.0, 0.0).astype(BF)


def params():
    return pltpu.CompilerParams(dimension_semantics=("arbitrary",), vmem_limit_bytes=VMEM)


def plain():
    return pltpu.CompilerParams(vmem_limit_bytes=VMEM)


def hub_kernel(hub_ref, x_ref, out_ref):
    hub_t = hub_ref[...].T
    lane = lax.broadcasted_iota(jnp.int32, (HUBD, ROWS), 1)
    hubs = jnp.dot(onehot(hub_t[:, 0:1] == lane), x_ref[...], preferred_element_type=F32).astype(BF)
    for s in range(PEERS):
        out_ref[s] = hubs


def halo_kernel(rows_ref, x_ref, out_ref):
    x = x_ref[...]
    rows_t = rows_ref[...].T
    lane = lax.broadcasted_iota(jnp.int32, (CAP, ROWS), 1)
    per = 8
    for block in range(PEERS // per):
        picks = jnp.concatenate(
            [onehot(rows_t[:, s : s + 1] == lane) for s in range(block * per, (block + 1) * per)], axis=0
        )
        got = jnp.dot(picks, x, preferred_element_type=F32).astype(BF)
        for n in range(per):
            out_ref[block * per + n] = got[n * CAP : (n + 1) * CAP, :]


def hub_rows_of(feats, hub_rows):
    return pl.pallas_call(
        hub_kernel,
        out_shape=pltpu.HBM((PEERS, HUBD, WIDTH), BF),
        compiler_params=plain(),
        name="hub_rows",
    )(hub_rows, feats)


def halo_rows_of(feats, send_rows):
    return pl.pallas_call(
        halo_kernel,
        out_shape=pltpu.HBM((PEERS, CAP, WIDTH), BF),
        compiler_params=plain(),
        cost_estimate=pl.CostEstimate(flops=3_000_000_000, bytes_accessed=3_000_000, transcendentals=0),
        name="halo_rows",
    )(send_rows, feats)


def count_kernel(idx_ref, xall_ref, *refs):
    agg_ref, rem_ref, ring_ref, loc_ref = refs[-4:]
    high = (LOCAL_HI + REM_HI) * GROUP
    row = lax.broadcasted_iota(jnp.int32, (LO, LO), 0).astype(F32).astype(BF)
    over = high - LO
    node = lax.broadcasted_iota(jnp.int32, (1, LO), 1) // DEG
    one = jnp.ones((LO, LO), BF)
    zero = jnp.zeros((LO, LO), BF)

    def spread(v, rows):
        return jnp.broadcast_to(v.astype(F32).astype(BF), (rows, LO))

    def build(g, carry):
        idx = idx_ref[pl.ds(g, 1), :]
        where_hi = (idx >> 8) * GROUP + node
        left = jnp.concatenate(
            [
                jnp.where(spread(where_hi, LO) == row, one, zero),
                jnp.where(spread(where_hi - LO, over) == row[0:over], one[0:over], zero[0:over]),
            ],
            axis=0,
        )
        low = jnp.where(spread(idx & (LO - 1), LO) == row, one, zero)
        counts = lax.dot_general(left, low, NT, preferred_element_type=F32).astype(BF)
        at = pl.ds(pl.multiple_of(g * GROUP, GROUP), GROUP)
        for h in range(LOCAL_HI):
            loc_ref[at, h * LO : (h + 1) * LO] = counts[h * GROUP : (h + 1) * GROUP, :]
        for h in range(REM_HI):
            r = (LOCAL_HI + h) * GROUP
            into, to = (ring_ref, h - FAR) if FAR <= h < 2 * FAR else (rem_ref, h % FAR + h // (2 * FAR) * FAR)
            into[at, to * LO : (to + 1) * LO] = counts[r : r + GROUP, :]
        return carry

    lax.fori_loop(0, TILE // GROUP, build, 0, unroll=UNROLL)
    agg_ref[...] = jnp.dot(loc_ref[...], xall_ref[...], preferred_element_type=F32)


def count_part(idx, feats, at, steps, before):
    rows = lambda n: pl.BlockSpec((TILE, n), lambda i: (i + at, 0))
    return pl.pallas_call(
        count_kernel,
        grid=(steps,),
        in_specs=[pl.BlockSpec((TILE // GROUP, LO), lambda i: (i + at, 0)), whole()]
        + [pl.BlockSpec(memory_space=pl.ANY)] * len(before),
        out_specs=[rows(WIDTH), rows(2 * FAR * LO), rows(FAR * LO)],
        out_shape=[
            pltpu.HBM((ROWS, WIDTH), F32), pltpu.HBM((ROWS, 2 * FAR * LO), BF), pltpu.HBM((ROWS, FAR * LO), BF),
        ],
        scratch_shapes=[pltpu.VMEM((TILE, ROWS), BF)],
        input_output_aliases={2: 0, 3: 1, 4: 2} if before else {},
        compiler_params=params(),
        cost_estimate=pl.CostEstimate(
            flops=5_000_000_000 * steps, bytes_accessed=5_000_000 * steps, transcendentals=0
        ),
        name="count_part",
    )(idx, feats, *before)


def soft(logits):
    scaled = logits / TEMPER
    e = jnp.exp(scaled - jnp.max(scaled, axis=-1, keepdims=True))
    return e / jnp.sum(e, axis=-1, keepdims=True)


def dense_kernel(
    agg_ref, ring_ref, x_ref, p0, p1, p2, p3, wself_ref, sfirst_ref, ssecond_ref, out_ref, base_ref, sh_ref, ps_ref
):
    acc = agg_ref[...]
    for n, part in enumerate((p0, p1, p2, p3)):
        acc = acc + jnp.dot(ring_ref[:, n * LO : (n + 1) * LO], part[...], preferred_element_type=F32)
    out_ref[...] = acc
    x = x_ref[...]
    base_ref[...] = jnp.dot(x, wself_ref[...], preferred_element_type=F32)
    hidden = jnp.maximum(jnp.dot(x, sfirst_ref[...], preferred_element_type=F32), 0.0).astype(BF)
    sh_ref[...] = hidden
    ps_ref[...] = soft(jnp.dot(hidden, ssecond_ref[...], preferred_element_type=F32))


def whole():
    return pl.BlockSpec(memory_space=pltpu.VMEM)


def once(shape):
    return pl.BlockSpec(shape, lambda i: (0,) * len(shape), pipeline_mode=pl.Buffered(1))


def hbm(x):
    return pltpu.with_memory_space_constraint(x, pltpu.HBM)


def tile(n):
    return pl.BlockSpec((TILE, n), lambda i: (i, 0))


def dense_part(agg, ring, feats, parts, w_self, s_first, s_second):
    return pl.pallas_call(
        dense_kernel,
        grid=(ROWS // TILE,),
        in_specs=[tile(WIDTH), tile(FAR * LO), tile(WIDTH)]
        + [once((LO, WIDTH))] * 4
        + [whole(), whole(), whole()],
        out_specs=[tile(WIDTH), tile(WIDTH), tile(WIDTH), tile(128)],
        out_shape=[
            pltpu.HBM((ROWS, WIDTH), F32), pltpu.HBM((ROWS, WIDTH), F32), pltpu.HBM((ROWS, WIDTH), BF),
            pltpu.HBM((ROWS, 128), F32),
        ],
        compiler_params=params(),
        cost_estimate=pl.CostEstimate(flops=3_000_000_000, bytes_accessed=10_000_000, transcendentals=0),
        name="dense_part",
    )(*map(hbm, (agg, ring, feats, *parts)), w_self, s_first, s_second)


def tail_kernel(
    scale, pos_ref, agg_ref, rem_ref, base_ref, sh_ref, ps_ref, x_ref, r_ref, p4, p5, p6, p7,
    wneigh_ref, whead_ref, ssecond_ref, hid_ref, keep_ref, send_ref, g_ref,
):
    step = pl.program_id(0)

    @pl.when(step == 0)
    def _():
        g_ref[...] = jnp.zeros_like(g_ref)

    first = PEERS * CAP
    acc = agg_ref[...] + jnp.dot(rem_ref[:, 0:first], r_ref[...], preferred_element_type=F32)
    for n, part in enumerate((p4, p5, p6, p7)):
        at = first + n * LO
        acc = acc + jnp.dot(rem_ref[:, at : at + LO], part[...], preferred_element_type=F32)
    agg = (acc / DEG).astype(BF)
    pre = base_ref[...] + jnp.dot(agg, wneigh_ref[...], preferred_element_type=F32)
    hidden = jnp.maximum(pre, 0.0).astype(BF)
    hid_ref[...] = hidden
    teach = soft(jnp.dot(hidden, whead_ref[...], preferred_element_type=F32))
    delta = (TEMPER * (ps_ref[...] - teach) * scale).astype(BF)
    sh = sh_ref[...]
    back = lax.dot_general(delta, ssecond_ref[...], NT, preferred_element_type=F32)
    back = jnp.where(sh.astype(F32) > 0.0, back, 0.0).astype(BF)
    first_grad = lax.dot_general(x_ref[...], back, TN, preferred_element_type=F32)
    for c in range(4):
        g_ref[c * WIDTH : (c + 1) * WIDTH, :] += first_grad[:, c * 128 : (c + 1) * 128]
    g_ref[4 * WIDTH : 5 * WIDTH, :] += lax.dot_general(sh, delta, TN, preferred_element_type=F32)

    @pl.when(step == pl.num_programs(0) - 1)
    def _():
        core = pos_ref[1]
        keep_ref[...] = g_ref[pl.ds(pl.multiple_of(core * HALF, 8), HALF), :]
        send_ref[...] = g_ref[pl.ds(pl.multiple_of((1 - core) * HALF, 8), HALF), :]


SMEM_SPEC = pl.BlockSpec(memory_space=pltpu.SMEM)


def tail_part(scale, pos, agg, rem, base, sh, ps, feats, got, parts, w_neigh, w_head, s_second):
    fixed = pl.BlockSpec((HALF, 128), lambda i: (0, 0))
    return pl.pallas_call(
        functools.partial(tail_kernel, scale),
        grid=(ROWS // TILE,),
        in_specs=[
            SMEM_SPEC, tile(WIDTH), tile(2 * FAR * LO), tile(WIDTH), tile(WIDTH), tile(128), tile(WIDTH),
            once((PEERS * CAP, WIDTH)),
        ]
        + [once((LO, WIDTH))] * 4
        + [whole(), whole(), whole()],
        out_specs=[tile(WIDTH), fixed, fixed],
        out_shape=[
            pltpu.HBM((ROWS, WIDTH), BF),
            jax.ShapeDtypeStruct((HALF, 128), F32),
            jax.ShapeDtypeStruct((HALF, 128), F32),
        ],
        scratch_shapes=[pltpu.VMEM((2 * HALF, 128), F32)],
        compiler_params=params(),
        cost_estimate=pl.CostEstimate(flops=10_000_000_000, bytes_accessed=30_000_000, transcendentals=0),
        name="tail_part",
    )(pos, *map(hbm, (agg, rem, base, sh, ps, feats, got, *parts)), w_neigh, w_head, s_second)


HALF = 5 * WIDTH // 2


def unpack_kernel(pos_ref, mine_ref, other_ref, first, second, g_ref):
    core = pos_ref[1]
    g_ref[pl.ds(pl.multiple_of(core * HALF, 16), HALF), :] = mine_ref[...].astype(F32)
    g_ref[pl.ds(pl.multiple_of((1 - core) * HALF, 16), HALF), :] = other_ref[...].astype(F32)
    for c in range(4):
        first[:, c * 128 : (c + 1) * 128] = g_ref[c * WIDTH : (c + 1) * WIDTH, :]
    second[...] = g_ref[4 * WIDTH : 5 * WIDTH, :]


def unpack(pos, mine, other):
    vmem = pl.BlockSpec(memory_space=pltpu.VMEM)
    return pl.pallas_call(
        unpack_kernel,
        in_specs=[SMEM_SPEC, vmem, vmem],
        out_specs=[vmem, vmem],
        out_shape=[jax.ShapeDtypeStruct((WIDTH, WIDTH), F32), jax.ShapeDtypeStruct((WIDTH, 128), F32)],
        scratch_shapes=[pltpu.VMEM((2 * HALF, 128), F32)],
        compiler_params=pltpu.CompilerParams(vmem_limit_bytes=16 << 20),
        name="unpack",
    )(pos, mine, other)


def shift(x, axis, n, k):
    return lax.ppermute(x, axis, [(i, (i + k) % n) for i in range(n)])


def swap(x):
    return lax.ppermute(x, "core", [(0, 1), (1, 0)])


def reduce_grads(pos, keep, send):
    total = keep + swap(send)
    plane = NY * NP * NX
    piece = HALF // plane
    part = jnp.sum(a2a(total, PLANE).reshape(plane, piece, 128), axis=0)
    part = jnp.sum(a2a(copies(part, NZ), "z").reshape(NZ, piece, 128), axis=0)
    mine = a2a(copies(part.astype(LAST), plane), PLANE)
    return unpack(pos, mine, swap(mine))


def remap(neighbours, y, c):
    hub = neighbours - ROWS - PEERS * CAP
    block = hub // LO
    other = ((block % 2) ^ c) * NY + (y - block // 2) % NY
    far = ROWS + PEERS * CAP + other * LO + hub % LO
    out = jnp.where(hub < 0, neighbours, far)
    return out.reshape(ROWS // GROUP, GROUP * DEG)


def a2a(x, axes):
    return lax.all_to_all(x, axes, split_axis=0, concat_axis=0, tiled=True)


def copies(x, n):
    return jnp.broadcast_to(x[None], (n,) + x.shape).reshape((n * x.shape[0],) + x.shape[1:])


def body(feats, send_rows, hub_rows, neighbours, w_self, w_neigh, w_head, s_first, s_second):
    y = lax.axis_index("y")
    c = lax.axis_index("core")
    pos = jnp.stack([y, c]).astype(jnp.int32)
    scale = 1.0 / float(ROWS * NY * NC * NZ * NP * NX) ** 0.5

    own = a2a(hub_rows_of(feats, hub_rows), DOM).reshape(LO, WIDTH)
    out = halo_rows_of(feats, send_rows[0])
    idx = remap(neighbours, y, c)
    counts = count_part(idx, feats, 0, FIRST, [])
    got = a2a(out, DOM)
    ring = [own] + [shift(own, "y", NY, k) for k in range(1, NY)]
    agg, rem, near = count_part(idx, feats, FIRST, ROWS // TILE - FIRST, counts)
    cross = [swap(r) for r in ring]
    agg, base, sh, ps = dense_part(agg, near, feats, ring, w_self, s_first, s_second)
    hidden, keep, send = tail_part(
        scale, pos, agg, rem, base, sh, ps, feats, got.reshape(PEERS * CAP, WIDTH), cross,
        w_neigh, w_head, s_second,
    )
    grad_first, grad_second = reduce_grads(pos, keep, send)
    return hidden, grad_first, grad_second


def solution(mesh):
    inner = Mesh(mesh.devices.reshape(NY, NC, NZ, NP, NX), ALL)
    return jax.shard_map(
        body,
        mesh=inner,
        in_specs=(P(ALL, None), P(ALL, None, None), P(ALL, None), P(ALL, None), P(), P(), P(), P(), P()),
        out_specs=(P(ALL, None), P(), P()),
        check_vma=False,
    )
```

```python
import functools

import jax
import jax.numpy as jnp
from jax import lax
from jax.experimental import pallas as pl
from jax.experimental.pallas import tpu as pltpu
from jax.sharding import Mesh
from jax.sharding import PartitionSpec as P

DEG = 16
TEMPER = 2.0
NY, NC, NZ, NP, NX = 4, 2, 4, 2, 4
ALL = ("y", "core", "z", "pair", "x")
DOM = ("z", "pair", "x")
PLANE = ("y", "pair", "x")
BF = jnp.bfloat16
F32 = jnp.float32
LAST = jnp.bfloat16
NT = (((1,), (1,)), ((), ()))
TN = (((0,), (0,)), ((), ()))

ROWS = 2048
WIDTH = 512
PEERS = 32
CAP = 32
HUBD = 8
LO = 256
LOCAL_HI = ROWS // LO
REM_HI = 12
FAR = 4
GROUP = 16
TILE = 512
VMEM = 30 << 20
UNROLL = 16
FIRST = 1


def onehot(cond):
    return jnp.where(cond, 1.0, 0.0).astype(BF)


def params():
    return pltpu.CompilerParams(dimension_semantics=("arbitrary",), vmem_limit_bytes=VMEM)


def plain():
    return pltpu.CompilerParams(vmem_limit_bytes=VMEM)


def hub_kernel(hub_ref, x_ref, out_ref):
    hub_t = hub_ref[...].T
    lane = lax.broadcasted_iota(jnp.int32, (HUBD, ROWS), 1)
    hubs = jnp.dot(onehot(hub_t[:, 0:1] == lane), x_ref[...], preferred_element_type=F32).astype(BF)
    for s in range(PEERS):
        out_ref[s] = hubs


def halo_kernel(rows_ref, x_ref, out_ref):
    x = x_ref[...]
    rows_t = rows_ref[...].T
    lane = lax.broadcasted_iota(jnp.int32, (CAP, ROWS), 1)
    per = 8
    for block in range(PEERS // per):
        picks = jnp.concatenate(
            [onehot(rows_t[:, s : s + 1] == lane) for s in range(block * per, (block + 1) * per)], axis=0
        )
        got = jnp.dot(picks, x, preferred_element_type=F32).astype(BF)
        for n in range(per):
            out_ref[block * per + n] = got[n * CAP : (n + 1) * CAP, :]


def hub_rows_of(feats, hub_rows):
    return pl.pallas_call(
        hub_kernel,
        out_shape=pltpu.HBM((PEERS, HUBD, WIDTH), BF),
        compiler_params=plain(),
        name="hub_rows",
    )(hub_rows, feats)


def halo_rows_of(feats, send_rows):
    return pl.pallas_call(
        halo_kernel,
        out_shape=pltpu.HBM((PEERS, CAP, WIDTH), BF),
        compiler_params=plain(),
        cost_estimate=pl.CostEstimate(flops=3_000_000_000, bytes_accessed=3_000_000, transcendentals=0),
        name="halo_rows",
    )(send_rows, feats)


def count_kernel(idx_ref, xall_ref, *refs):
    agg_ref, rem_ref, ring_ref, loc_ref = refs[-4:]
    high = (LOCAL_HI + REM_HI) * GROUP
    row = lax.broadcasted_iota(jnp.int32, (LO, LO), 0).astype(F32).astype(BF)
    over = high - LO
    node = lax.broadcasted_iota(jnp.int32, (1, LO), 1) // DEG
    one = jnp.ones((LO, LO), BF)
    zero = jnp.zeros((LO, LO), BF)

    def spread(v, rows):
        return jnp.broadcast_to(v.astype(F32).astype(BF), (rows, LO))

    def build(g, carry):
        idx = idx_ref[pl.ds(g, 1), :]
        where_hi = (idx >> 8) * GROUP + node
        left = jnp.concatenate(
            [
                jnp.where(spread(where_hi, LO) == row, one, zero),
                jnp.where(spread(where_hi - LO, over) == row[0:over], one[0:over], zero[0:over]),
            ],
            axis=0,
        )
        low = jnp.where(spread(idx & (LO - 1), LO) == row, one, zero)
        counts = lax.dot_general(left, low, NT, preferred_element_type=F32).astype(BF)
        at = pl.ds(pl.multiple_of(g * GROUP, GROUP), GROUP)
        for h in range(LOCAL_HI):
            loc_ref[at, h * LO : (h + 1) * LO] = counts[h * GROUP : (h + 1) * GROUP, :]
        for h in range(REM_HI):
            r = (LOCAL_HI + h) * GROUP
            into, to = (ring_ref, h - FAR) if FAR <= h < 2 * FAR else (rem_ref, h % FAR + h // (2 * FAR) * FAR)
            into[at, to * LO : (to + 1) * LO] = counts[r : r + GROUP, :]
        return carry

    lax.fori_loop(0, TILE // GROUP, build, 0, unroll=UNROLL)
    agg_ref[...] = jnp.dot(loc_ref[...], xall_ref[...], preferred_element_type=F32)


def count_part(idx, feats, at, steps, before):
    rows = lambda n: pl.BlockSpec((TILE, n), lambda i: (i + at, 0))
    return pl.pallas_call(
        count_kernel,
        grid=(steps,),
        in_specs=[pl.BlockSpec((TILE // GROUP, LO), lambda i: (i + at, 0)), whole()]
        + [pl.BlockSpec(memory_space=pl.ANY)] * len(before),
        out_specs=[rows(WIDTH), rows(2 * FAR * LO), rows(FAR * LO)],
        out_shape=[
            pltpu.HBM((ROWS, WIDTH), F32), pltpu.HBM((ROWS, 2 * FAR * LO), BF), pltpu.HBM((ROWS, FAR * LO), BF),
        ],
        scratch_shapes=[pltpu.VMEM((TILE, ROWS), BF)],
        input_output_aliases={2: 0, 3: 1, 4: 2} if before else {},
        compiler_params=params(),
        cost_estimate=pl.CostEstimate(
            flops=5_000_000_000 * steps, bytes_accessed=5_000_000 * steps, transcendentals=0
        ),
        name="count_part",
    )(idx, feats, *before)


def soft(logits):
    scaled = logits / TEMPER
    e = jnp.exp(scaled - jnp.max(scaled, axis=-1, keepdims=True))
    return e / jnp.sum(e, axis=-1, keepdims=True)


def dense_kernel(
    agg_ref, ring_ref, x_ref, p0, p1, p2, p3, wself_ref, sfirst_ref, ssecond_ref, out_ref, base_ref, sh_ref, ps_ref
):
    acc = agg_ref[...]
    for n, part in enumerate((p0, p1, p2, p3)):
        acc = acc + jnp.dot(ring_ref[:, n * LO : (n + 1) * LO], part[...], preferred_element_type=F32)
    out_ref[...] = acc
    x = x_ref[...]
    base_ref[...] = jnp.dot(x, wself_ref[...], preferred_element_type=F32)
    hidden = jnp.maximum(jnp.dot(x, sfirst_ref[...], preferred_element_type=F32), 0.0).astype(BF)
    sh_ref[...] = hidden
    ps_ref[...] = soft(jnp.dot(hidden, ssecond_ref[...], preferred_element_type=F32))


def whole():
    return pl.BlockSpec(memory_space=pltpu.VMEM)


def once(shape):
    return pl.BlockSpec(shape, lambda i: (0,) * len(shape), pipeline_mode=pl.Buffered(1))


def hbm(x):
    return pltpu.with_memory_space_constraint(x, pltpu.HBM)


def tile(n):
    return pl.BlockSpec((TILE, n), lambda i: (i, 0))


def dense_part(agg, ring, feats, parts, w_self, s_first, s_second):
    return pl.pallas_call(
        dense_kernel,
        grid=(ROWS // TILE,),
        in_specs=[tile(WIDTH), tile(FAR * LO), tile(WIDTH)]
        + [once((LO, WIDTH))] + [whole()] * 3
        + [whole(), whole(), whole()],
        out_specs=[tile(WIDTH), tile(WIDTH), tile(WIDTH), tile(128)],
        out_shape=[
            pltpu.HBM((ROWS, WIDTH), F32), pltpu.HBM((ROWS, WIDTH), F32), pltpu.HBM((ROWS, WIDTH), BF),
            pltpu.HBM((ROWS, 128), F32),
        ],
        compiler_params=params(),
        cost_estimate=pl.CostEstimate(flops=3_000_000_000, bytes_accessed=10_000_000, transcendentals=0),
        name="dense_part",
    )(*map(hbm, (agg, ring, feats, parts[0])), *parts[1:], w_self, s_first, s_second)


def tail_kernel(
    scale, pos_ref, agg_ref, rem_ref, base_ref, sh_ref, ps_ref, x_ref, r_ref, p4, p5, p6, p7,
    wneigh_ref, whead_ref, ssecond_ref, hid_ref, keep_ref, send_ref, g_ref,
):
    step = pl.program_id(0)

    @pl.when(step == 0)
    def _():
        g_ref[...] = jnp.zeros_like(g_ref)

    first = PEERS * CAP
    acc = agg_ref[...] + jnp.dot(rem_ref[:, 0:first], r_ref[...], preferred_element_type=F32)
    for n, part in enumerate((p4, p5, p6, p7)):
        at = first + n * LO
        acc = acc + jnp.dot(rem_ref[:, at : at + LO], part[...], preferred_element_type=F32)
    agg = (acc / DEG).astype(BF)
    pre = base_ref[...] + jnp.dot(agg, wneigh_ref[...], preferred_element_type=F32)
    hidden = jnp.maximum(pre, 0.0).astype(BF)
    hid_ref[...] = hidden
    teach = soft(jnp.dot(hidden, whead_ref[...], preferred_element_type=F32))
    delta = (TEMPER * (ps_ref[...] - teach) * scale).astype(BF)
    sh = sh_ref[...]
    back = lax.dot_general(delta, ssecond_ref[...], NT, preferred_element_type=F32)
    back = jnp.where(sh.astype(F32) > 0.0, back, 0.0).astype(BF)
    first_grad = lax.dot_general(x_ref[...], back, TN, preferred_element_type=F32)
    for c in range(4):
        g_ref[c * WIDTH : (c + 1) * WIDTH, :] += first_grad[:, c * 128 : (c + 1) * 128]
    g_ref[4 * WIDTH : 5 * WIDTH, :] += lax.dot_general(sh, delta, TN, preferred_element_type=F32)

    @pl.when(step == pl.num_programs(0) - 1)
    def _():
        core = pos_ref[1]
        keep_ref[...] = g_ref[pl.ds(pl.multiple_of(core * HALF, 8), HALF), :]
        send_ref[...] = g_ref[pl.ds(pl.multiple_of((1 - core) * HALF, 8), HALF), :]


SMEM_SPEC = pl.BlockSpec(memory_space=pltpu.SMEM)


def tail_part(scale, pos, agg, rem, base, sh, ps, feats, got, parts, w_neigh, w_head, s_second):
    fixed = pl.BlockSpec((HALF, 128), lambda i: (0, 0))
    return pl.pallas_call(
        functools.partial(tail_kernel, scale),
        grid=(ROWS // TILE,),
        in_specs=[
            SMEM_SPEC, tile(WIDTH), tile(2 * FAR * LO), tile(WIDTH), tile(WIDTH), tile(128), tile(WIDTH),
            whole(),
        ]
        + [once((LO, WIDTH))] + [whole()] * 3
        + [whole(), whole(), whole()],
        out_specs=[tile(WIDTH), fixed, fixed],
        out_shape=[
            pltpu.HBM((ROWS, WIDTH), BF),
            jax.ShapeDtypeStruct((HALF, 128), F32),
            jax.ShapeDtypeStruct((HALF, 128), F32),
        ],
        scratch_shapes=[pltpu.VMEM((2 * HALF, 128), F32)],
        compiler_params=params(),
        cost_estimate=pl.CostEstimate(flops=10_000_000_000, bytes_accessed=30_000_000, transcendentals=0),
        name="tail_part",
    )(pos, *map(hbm, (agg, rem, base, sh, ps, feats)), got, hbm(parts[0]), *parts[1:], w_neigh, w_head, s_second)


HALF = 5 * WIDTH // 2


def unpack_kernel(pos_ref, mine_ref, other_ref, first, second, g_ref):
    core = pos_ref[1]
    g_ref[pl.ds(pl.multiple_of(core * HALF, 16), HALF), :] = mine_ref[...].astype(F32)
    g_ref[pl.ds(pl.multiple_of((1 - core) * HALF, 16), HALF), :] = other_ref[...].astype(F32)
    for c in range(4):
        first[:, c * 128 : (c + 1) * 128] = g_ref[c * WIDTH : (c + 1) * WIDTH, :]
    second[...] = g_ref[4 * WIDTH : 5 * WIDTH, :]


def unpack(pos, mine, other):
    vmem = pl.BlockSpec(memory_space=pltpu.VMEM)
    return pl.pallas_call(
        unpack_kernel,
        in_specs=[SMEM_SPEC, vmem, vmem],
        out_specs=[vmem, vmem],
        out_shape=[jax.ShapeDtypeStruct((WIDTH, WIDTH), F32), jax.ShapeDtypeStruct((WIDTH, 128), F32)],
        scratch_shapes=[pltpu.VMEM((2 * HALF, 128), F32)],
        compiler_params=pltpu.CompilerParams(vmem_limit_bytes=16 << 20),
        name="unpack",
    )(pos, mine, other)


def shift(x, axis, n, k):
    return lax.ppermute(x, axis, [(i, (i + k) % n) for i in range(n)])


def swap(x):
    return lax.ppermute(x, "core", [(0, 1), (1, 0)])


def reduce_grads(pos, keep, send):
    total = keep + swap(send)
    plane = NY * NP * NX
    piece = HALF // plane
    part = jnp.sum(a2a(total, PLANE).reshape(plane, piece, 128), axis=0)
    part = jnp.sum(a2a(copies(part, NZ), "z").reshape(NZ, piece, 128), axis=0)
    mine = a2a(copies(part.astype(LAST), plane), PLANE)
    return unpack(pos, mine, swap(mine))


def remap(neighbours, y, c):
    hub = neighbours - ROWS - PEERS * CAP
    block = hub // LO
    other = ((block % 2) ^ c) * NY + (y - block // 2) % NY
    far = ROWS + PEERS * CAP + other * LO + hub % LO
    out = jnp.where(hub < 0, neighbours, far)
    return out.reshape(ROWS // GROUP, GROUP * DEG)


def a2a(x, axes):
    return lax.all_to_all(x, axes, split_axis=0, concat_axis=0, tiled=True)


def copies(x, n):
    return jnp.broadcast_to(x[None], (n,) + x.shape).reshape((n * x.shape[0],) + x.shape[1:])


def body(feats, send_rows, hub_rows, neighbours, w_self, w_neigh, w_head, s_first, s_second):
    y = lax.axis_index("y")
    c = lax.axis_index("core")
    pos = jnp.stack([y, c]).astype(jnp.int32)
    scale = 1.0 / float(ROWS * NY * NC * NZ * NP * NX) ** 0.5

    own = a2a(hub_rows_of(feats, hub_rows), DOM).reshape(LO, WIDTH)
    out = halo_rows_of(feats, send_rows[0])
    idx = remap(neighbours, y, c)
    counts = count_part(idx, feats, 0, FIRST, [])
    got = a2a(out, DOM)
    ring = [own] + [shift(own, "y", NY, k) for k in range(1, NY)]
    agg, rem, near = count_part(idx, feats, FIRST, ROWS // TILE - FIRST, counts)
    cross = [swap(r) for r in ring]
    agg, base, sh, ps = dense_part(agg, near, feats, ring, w_self, s_first, s_second)
    hidden, keep, send = tail_part(
        scale, pos, agg, rem, base, sh, ps, feats, got.reshape(PEERS * CAP, WIDTH), cross,
        w_neigh, w_head, s_second,
    )
    grad_first, grad_second = reduce_grads(pos, keep, send)
    return hidden, grad_first, grad_second


def solution(mesh):
    inner = Mesh(mesh.devices.reshape(NY, NC, NZ, NP, NX), ALL)
    return jax.shard_map(
        body,
        mesh=inner,
        in_specs=(P(ALL, None), P(ALL, None, None), P(ALL, None), P(ALL, None), P(), P(), P(), P(), P()),
        out_specs=(P(ALL, None), P(), P()),
        check_vma=False,
    )
```
